32 devices in a mesh: energy: 8 (over y, x, core), section: 4 (over z).
Axes of the slice: x: 2, y: 2, z: 4, core: 2. Of those that a mesh axis runs over, the one named last changes fastest.
Arguments:
- self_in: float32 [32, 4, 2, 256, 256], P('energy', 'section'), as said below
- onsite: float32 [4, 256], P('section'), may hold values from -1 to 1
- within: float32 [4, 256, 256], P('section'), may hold values from -0.09375 to 0.09375
- between: float32 [4, 256, 256], P('section'), as said below
- coupling: float32 [4, 256, 256], P('section'), may hold values from -1 to 1
- groups: int32 [4, 256], P('section'), may hold values from 0 to 3
- offsets: int32 [3], replicated, may hold values from 1 to 2, as said below
- strength: float32 [3], replicated, may hold values from 0.3 to 1
Outputs:
- green: float32 [32, 4, 2, 256, 256], P('energy', 'section')
- self_out: float32 [32, 4, 2, 256, 256], P('energy', 'section')
The draws below stay inside these ranges and needn't reach their ends.
Inputs may be any that keep to these rules, and one draw needn't show every extreme that they name: `offsets`: every entry lies between 1 and 2, and one entry equals 2. `self_in`: imaginary parts of diagonal entries lie between -0.02 and -0.002, real parts of diagonal entries between -0.3 and 0.3; off-diagonal entries lie between -0.01 and 0.01. `between`: diagonal entries lie between 1.4 and 2.0; off-diagonal entries are at most 1.12 / sqrt(256) in magnitude.
All inputs are finite; a program needn't handle non-finite values.
Results may differ from the reference program's by a relative error of at most 0.0001.
Values sent between devices are 32-bit elements; how exact they have to be, the bound alone decides.
A program may use at most 128 MiB of HBM per device.

```python
import math
import jax
import jax.numpy as jnp
from jax import lax

B = 256
NEWTON = 3
MODES = 3
GROUPS = 4
OFF_MAX = 2
ENERGIES = 32
SLABS = 4


def draw_self_in(key, part):
    shape = (ENERGIES, SLABS, 2, B, B)
    first_key = jax.random.fold_in(key, 11)
    second_key = jax.random.fold_in(key, 12)
    third_key = jax.random.fold_in(key, 13)
    spread = jnp.clip(0.004 * jax.random.normal(first_key, shape, jnp.float32), -0.01, 0.01)
    real_diag = jax.random.uniform(second_key, (ENERGIES, SLABS, B), jnp.float32, -0.3, 0.3)
    imag_diag = jax.random.uniform(third_key, (ENERGIES, SLABS, B), jnp.float32, -0.02, -0.002)
    identity = jnp.eye(B, dtype=jnp.float32)
    diagonal = jnp.stack([real_diag, imag_diag], axis=2)[..., :, None] * identity
    return spread * (1.0 - identity) + diagonal


def draw_between(key, part):
    diag_key = jax.random.fold_in(key, 31)
    rest_key = jax.random.fold_in(key, 32)
    identity = jnp.eye(B, dtype=jnp.float32)
    diag_values = jax.random.uniform(diag_key, (SLABS, B), jnp.float32, 1.4, 2.0)
    scale = 0.28 * B ** (-0.5)
    rest = jnp.clip(scale * jax.random.normal(rest_key, (SLABS, B, B), jnp.float32), -4.0 * scale, 4.0 * scale)
    return rest * (1.0 - identity) + diag_values[:, :, None] * identity


def draw_offsets(key, part):
    values = jax.random.randint(jax.random.fold_in(key, 21), (MODES,), 1, OFF_MAX + 1)
    chosen = jax.random.randint(jax.random.fold_in(key, 22), (), 0, MODES)
    return jnp.where(jnp.arange(MODES) == chosen, OFF_MAX, values).astype(jnp.int32)


def touch_ends(values, stream_key, low, largest):
    extent = values.shape
    index_at = [jax.random.randint(jax.random.fold_in(stream_key, axis), (), 0, extent[axis]) for axis in range(len(extent))]
    values = values.at[tuple(index_at)].set(low)
    longest = extent.index(max(extent))
    index_at[longest] = (index_at[longest] + 1) % extent[longest]
    return values.at[tuple(index_at)].set(largest)


def shard_levels(key, shape, cuts, low, largest):
    loudness, own = 1.0, jax.random.fold_in(key, 6)
    for axis_at, parts in cuts:
        steps = jnp.exp(jax.random.uniform(jax.random.fold_in(own, axis_at), (parts,), jnp.float32, low / len(cuts), largest / len(cuts)))
        loudness = loudness * jnp.repeat(steps, shape[axis_at] // parts).reshape([-1 if axis == axis_at else 1 for axis in range(len(shape))])
    return loudness


def normal_values(key, shape, scale, reach, shards=(), kind=jnp.bfloat16):
    level = shard_levels(key, shape, shards, -0.22, 0.18) if shards else 1.0
    array = jax.random.normal(key, shape, jnp.float32) * scale * level
    return jnp.minimum(jnp.maximum(array, -reach), reach).astype(kind)


def setup_inputs(seed: int = 0) -> dict:
    arg_keys = jax.random.split(jax.random.key(seed), 9)
    self_in = draw_self_in(jax.random.fold_in(arg_keys[8], 71), 0)
    onsite = jnp.clip(jax.random.uniform(arg_keys[1], (SLABS, B), jnp.float32, -1.0, 1.0) * shard_levels(arg_keys[1], (SLABS, B), ((0, 4),), -0.4, 0.0), -1.0, 1.0)
    within = normal_values(arg_keys[2], (SLABS, B, B), (16 * B) ** -0.5, 0.09375, ((0, 4),), jnp.float32)
    between = draw_between(jax.random.fold_in(arg_keys[8], 71), 0)
    coupling = normal_values(arg_keys[4], (SLABS, B, B), 0.18, 1.0, ((0, 4),), jnp.float32)
    groups = touch_ends(jax.random.randint(arg_keys[5], (SLABS, B), 0, GROUPS), jax.random.fold_in(arg_keys[5], 1), 0, GROUPS - 1).astype(jnp.int32)
    offsets = draw_offsets(jax.random.fold_in(arg_keys[8], 71), 0)
    strength = jnp.clip(jnp.exp(jax.random.uniform(arg_keys[7], (MODES,), jnp.float32, math.log(0.3), math.log(1.0))), 0.3, 1.0)
    return {"self_in": self_in, "onsite": onsite, "within": within, "between": between, "coupling": coupling, "groups": groups, "offsets": offsets, "strength": strength}


HIGH = lax.Precision.HIGHEST
ETA = 1.0
CONTACT = 0.6


def multiply(left, right):
    return jnp.einsum("...ij,...jk->...ik", left, right, precision=HIGH)


def product(left, right):
    real_a, imag_a = left[..., 0, :, :], left[..., 1, :, :]
    real_b, imag_b = right[..., 0, :, :], right[..., 1, :, :]
    return jnp.stack([multiply(real_a, real_b) - multiply(imag_a, imag_b),
                      multiply(real_a, imag_b) + multiply(imag_a, real_b)], axis=-3)


def times_real(field, matrix):
    return jnp.einsum("...ij,jk->...ik", field, matrix, precision=HIGH)


def real_times(matrix, field):
    return jnp.einsum("ij,...jk->...ik", matrix, field, precision=HIGH)


def newton(system):
    sys_re, sys_im = system[..., 0, :, :], system[..., 1, :, :]
    real_c = jnp.diagonal(sys_re, axis1=-2, axis2=-1)
    imag_c = jnp.diagonal(sys_im, axis1=-2, axis2=-1)
    modulus = real_c * real_c + imag_c * imag_c
    inv_re = real_c / modulus
    inv_im = -imag_c / modulus
    half_re = inv_re[..., :, None] * sys_re - inv_im[..., :, None] * sys_im
    half_im = inv_re[..., :, None] * sys_im + inv_im[..., :, None] * sys_re
    full_re = half_re * inv_re[..., None, :] - half_im * inv_im[..., None, :]
    full_im = half_re * inv_im[..., None, :] + half_im * inv_re[..., None, :]
    identity = jnp.eye(system.shape[-1], dtype=jnp.float32)
    iterate = jnp.stack([2.0 * inv_re[..., :, None] * identity - full_re,
                         2.0 * inv_im[..., :, None] * identity - full_im], axis=-3)
    for sweep in range(NEWTON - 1):
        iterate = 2.0 * iterate - product(iterate, product(system, iterate))
    return iterate


def local_inverse(energy, hamil, sigma, previous, hop):
    identity = jnp.eye(hamil.shape[-1], dtype=jnp.float32)
    left = real_times(hop.T, times_real(previous, hop))
    sys_re = energy[..., None, None] * identity - hamil - sigma[..., 0, :, :] - left[..., 0, :, :]
    sys_im = ETA * identity - sigma[..., 1, :, :] - left[..., 1, :, :]
    return newton(jnp.stack([sys_re, sys_im], axis=-3))


def refine(local_green, incoming):
    return local_green + product(local_green, product(incoming, local_green))


def sandwich(hop, green):
    return times_real(real_times(hop, green), hop.T)


def reference(self_in, onsite, within, between, coupling, groups, offsets, strength):
    width = onsite.shape[1]
    identity = jnp.eye(width, dtype=jnp.float32)
    hams = onsite[:, :, None] * identity + 0.5 * (within + jnp.swapaxes(within, 1, 2))
    energies = -1.0 + (2 * jnp.arange(ENERGIES, dtype=jnp.int32) + 1).astype(jnp.float32) / ENERGIES
    contact = jnp.stack([jnp.zeros((width, width), jnp.float32), -CONTACT * identity])

    def one_energy(inputs):
        energy, sigma_all = inputs

        def forward(previous, items):
            hamil, hop, sigma = items
            local_green = local_inverse(energy, hamil, sigma, previous, hop)
            return local_green, local_green

        _, locals_all = lax.scan(forward, contact, (hams, between, sigma_all))

        def backward(incoming, items):
            local_green, hop = items
            full = refine(local_green, incoming)
            return sandwich(hop, full), full

        _, greens = lax.scan(backward, jnp.zeros((2, width, width), jnp.float32),
                             (locals_all, between), reverse=True)
        return greens

    green = lax.map(one_energy, (energies, self_in))
    padded = jnp.pad(green, ((OFF_MAX, OFF_MAX), (0, 0), (0, 0), (0, 0), (0, 0)))
    summed = jnp.zeros_like(green)
    for mode in range(MODES):
        shift = offsets[mode].astype(jnp.int32)
        lower = lax.dynamic_slice_in_dim(padded, (OFF_MAX - shift).astype(jnp.int32), ENERGIES, 0)
        upper = lax.dynamic_slice_in_dim(padded, (OFF_MAX + shift).astype(jnp.int32), ENERGIES, 0)
        summed = summed + strength[mode] * (lower + upper)
    mats = jnp.where(groups[:, :, None] == groups[:, None, :], coupling, jnp.float32(0.0))
    first = jnp.einsum("sab,eszbc->eszac", mats, summed, precision=HIGH)
    self_out = jnp.einsum("eszac,sdc->eszad", first, mats, precision=HIGH)
    return green, self_out
```

```python
import functools

import jax
import jax.numpy as jnp
from jax import lax
from jax.experimental import pallas as pl
from jax.experimental.pallas import tpu as pltpu
from jax.sharding import PartitionSpec as P

NEWTON = 3
ETA = 1.0
CONTACT = 0.6
REACH = 2

F32 = jnp.float32
BF16 = jnp.bfloat16
MESH = pl.DeviceIdType.MESH


def split(value):
    high = value.astype(BF16)
    return high, (value - high.astype(F32)).astype(BF16)


def join(pieces, axis):
    return tuple(jnp.concatenate(parts, axis=axis) for parts in zip(*pieces))


def dot(left, right):
    return jnp.dot(left, right, preferred_element_type=F32)


def matmul(left, right):
    (left_h, left_l), (right_h, right_l) = left, right
    return dot(left_h, right_h) + (dot(left_h, right_l) + dot(left_l, right_h))


def minus(pair):
    return tuple(-part for part in pair)


def complex_product(left, right):
    size = left[0][0].shape[0]
    rows = join(left, 1)
    columns = join([join([right[0], right[1]], 1), join([minus(right[1]), right[0]], 1)], 0)
    result = matmul(rows, columns)
    return result[:, :size], result[:, size:]


def congruence(first, field, second):
    size = first[0].shape[0]
    half = matmul(join(field, 0), second)
    half = join([split(half[:size]), split(half[size:])], 1)
    result = matmul(first, half)
    return result[:, :size], result[:, size:]


def kernel(
    energies, offsets, strength, self_in, onsite, within, between, coupling, groups,
    green, self_out,
    hamil, hops, mats, local, came_f, came_b, sent_b, halo,
    send_f, recv_f, send_b, recv_b, send_h, recv_h,
):
    count, width = self_in.shape[0], self_in.shape[3]
    sections, place = lax.axis_size("section"), lax.axis_index("section")
    spans, seat = lax.axis_size("energy"), lax.axis_index("energy")
    has_prev, has_next = place > 0, place < sections - 1
    has_low, has_high = seat > 0, seat < spans - 1
    last = sections - 1

    barrier = pltpu.get_barrier_semaphore()
    for present, target in (
        (has_prev, {"section": place - 1}),
        (has_next, {"section": place + 1}),
        (has_low, {"energy": seat - 1}),
        (has_high, {"energy": seat + 1}),
    ):
        @pl.when(present)
        def _():
            pl.semaphore_signal(barrier, inc=1, device_id=target, device_id_type=MESH)

    eye = (
        lax.broadcasted_iota(jnp.int32, (width, width), 0)
        == lax.broadcasted_iota(jnp.int32, (width, width), 1)
    )
    hamil[...] = jnp.where(eye, onsite[0:1, :], 0.0) + 0.5 * (within[0] + within[0].T)
    hop = between[0]
    hops[0], hops[1] = split(hop)
    hops[2], hops[3] = split(hop.T)
    row_group = jnp.broadcast_to(groups[0:1, :].astype(F32), (width, width))
    mat = jnp.where(row_group == row_group.T, coupling[0], 0.0)
    mats[0], mats[1] = split(mat)
    mats[2], mats[3] = split(mat.T)

    @pl.when(place == 0)
    def _():
        for index in range(count):
            came_f[index, 0] = jnp.zeros((width, width), F32)
            came_f[index, 1] = jnp.where(eye, -CONTACT, 0.0)

    @pl.when(seat == 0)
    def _():
        halo[0:REACH] = jnp.zeros((REACH, 2, width, width), F32)

    @pl.when(seat == spans - 1)
    def _():
        halo[REACH : 2 * REACH] = jnp.zeros((REACH, 2, width, width), F32)

    peers = sum(present.astype(jnp.int32) for present in (has_prev, has_next, has_low, has_high))
    pl.semaphore_wait(barrier, peers)

    def forward_copy(index):
        return pltpu.make_async_remote_copy(
            src_ref=local.at[index], dst_ref=came_f.at[index],
            send_sem=send_f.at[index], recv_sem=recv_f.at[index],
            device_id={"section": place + 1}, device_id_type=MESH,
        )

    def backward_copy(index):
        return pltpu.make_async_remote_copy(
            src_ref=sent_b.at[index], dst_ref=came_b.at[index],
            send_sem=send_b.at[index], recv_sem=recv_b.at[index],
            device_id={"section": place - 1}, device_id_type=MESH,
        )

    def halo_up(index):
        slot = index - (count - REACH)
        return pltpu.make_async_remote_copy(
            src_ref=green.at[index, 0], dst_ref=halo.at[slot],
            send_sem=send_h.at[slot], recv_sem=recv_h.at[slot],
            device_id={"energy": seat + 1}, device_id_type=MESH,
        )

    def halo_down(index):
        slot = index + REACH
        return pltpu.make_async_remote_copy(
            src_ref=green.at[index, 0], dst_ref=halo.at[slot],
            send_sem=send_h.at[slot], recv_sem=recv_h.at[slot],
            device_id={"energy": seat - 1}, device_id_type=MESH,
        )

    def forward(index):
        @pl.when(has_prev)
        def _():
            forward_copy(index).wait_recv()

        field = (split(came_f[index, 0]), split(came_f[index, 1]))
        left_re, left_im = congruence(
            (hops[2], hops[3]), field, (hops[0], hops[1])
        )
        sys_re = jnp.where(eye, energies[index], 0.0) - hamil[...] - self_in[index, 0, 0] - left_re
        sys_im = jnp.where(eye, ETA, 0.0) - self_in[index, 0, 1] - left_im
        diag_re = jnp.where(eye, sys_re, 0.0)
        diag_im = jnp.where(eye, sys_im, 0.0)
        inverses = []
        for axis in (1, 0):
            real_c = jnp.sum(diag_re, axis=axis, keepdims=True)
            imag_c = jnp.sum(diag_im, axis=axis, keepdims=True)
            modulus = real_c * real_c + imag_c * imag_c
            inverses.append((real_c / modulus, -imag_c / modulus))
        (col_re, col_im), (row_re, row_im) = inverses
        half_re = col_re * sys_re - col_im * sys_im
        half_im = col_re * sys_im + col_im * sys_re
        it_re = jnp.where(eye, 2.0 * col_re, 0.0) - (half_re * row_re - half_im * row_im)
        it_im = jnp.where(eye, 2.0 * col_im, 0.0) - (half_re * row_im + half_im * row_re)
        system = (split(sys_re), split(sys_im))
        for _ in range(NEWTON - 1):
            iterate = (split(it_re), split(it_im))
            mid_re, mid_im = complex_product(system, iterate)
            out_re, out_im = complex_product(iterate, (split(mid_re), split(mid_im)))
            it_re, it_im = 2.0 * it_re - out_re, 2.0 * it_im - out_im
        local[index, 0] = it_re
        local[index, 1] = it_im

        @pl.when(has_next)
        def _():
            forward_copy(index).start()

    def backward(index):
        @pl.when(has_next)
        def _():
            backward_copy(index).wait_recv()
            base_re, base_im = local[index, 0], local[index, 1]
            base = (split(base_re), split(base_im))
            incoming = (split(came_b[index, 0]), split(came_b[index, 1]))
            mid_re, mid_im = complex_product(incoming, base)
            out_re, out_im = complex_product(base, (split(mid_re), split(mid_im)))
            green[index, 0, 0] = base_re + out_re
            green[index, 0, 1] = base_im + out_im

        @pl.when(place == last)
        def _():
            green[index, 0] = local[index]

        @pl.when(has_prev)
        def _():
            field = (split(green[index, 0, 0]), split(green[index, 0, 1]))
            out_re, out_im = congruence((hops[0], hops[1]), field, (hops[2], hops[3]))
            sent_b[index, 0] = out_re
            sent_b[index, 1] = out_im
            backward_copy(index).start()

        @pl.when(has_high & (index >= count - REACH))
        def _():
            halo_up(index).start()

        @pl.when(has_low & (index < REACH))
        def _():
            halo_down(index).start()

    def turn(step, carry):
        ahead = step - place
        back = step - 2 * last + place

        @pl.when((ahead >= 0) & (ahead < count))
        def _():
            forward(ahead)

        @pl.when((back >= 0) & (back < count))
        def _():
            backward(back)

        return carry

    lax.fori_loop(0, count + 2 * last, turn, 0)

    near = jnp.float32(0.0)
    far = jnp.float32(0.0)
    for mode in range(offsets.shape[0]):
        near = near + jnp.where(offsets[mode] == 1, strength[mode], 0.0)
        far = far + jnp.where(offsets[mode] == 2, strength[mode], 0.0)

    @pl.when(has_high)
    def _():
        for slot in range(REACH):
            halo_down(slot).wait_recv()

    def block(index, part):
        if index < 0:
            return halo[index + REACH, part]
        if index >= count:
            return halo[index - count + REACH, part]
        return green[index, 0, part]

    first, second = (mats[0], mats[1]), (mats[2], mats[3])
    waited = [False]
    for index in reversed(range(count)):
        if index < REACH and not waited[0]:
            waited[0] = True

            @pl.when(has_low)
            def _():
                for slot in range(REACH):
                    halo_up(count - REACH + slot).wait_recv()

        field = tuple(
            split(
                near * (block(index - 1, part) + block(index + 1, part))
                + far * (block(index - 2, part) + block(index + 2, part))
            )
            for part in range(2)
        )
        out_re, out_im = congruence(first, field, second)
        self_out[index, 0, 0] = out_re
        self_out[index, 0, 1] = out_im

    @pl.when(has_next)
    def _():
        for index in range(count):
            forward_copy(index).wait_send()

    @pl.when(has_prev)
    def _():
        for index in range(count):
            backward_copy(index).wait_send()

    @pl.when(has_high)
    def _():
        for slot in range(REACH):
            halo_up(count - REACH + slot).wait_send()

    @pl.when(has_low)
    def _():
        for slot in range(REACH):
            halo_down(slot).wait_send()


def per_device(self_in, onsite, within, between, coupling, groups, offsets, strength):
    count, width = self_in.shape[0], self_in.shape[3]
    total = count * lax.axis_size("energy")
    first_index = lax.axis_index("energy") * count
    energies = (
        -1.0
        + (2 * (first_index + jnp.arange(count, dtype=jnp.int32)) + 1).astype(jnp.float32) / total
    )
    smem = pl.BlockSpec(memory_space=pltpu.SMEM)
    vmem = pl.BlockSpec(memory_space=pltpu.VMEM)
    shape = jax.ShapeDtypeStruct(self_in.shape, F32)
    dma = pltpu.SemaphoreType.DMA
    return pl.pallas_call(
        kernel,
        out_shape=(shape, shape),
        in_specs=[smem] * 3 + [vmem] * 6,
        out_specs=(vmem, vmem),
        scratch_shapes=[
            pltpu.VMEM((width, width), F32),
            pltpu.VMEM((4, width, width), BF16),
            pltpu.VMEM((4, width, width), BF16),
            pltpu.VMEM((count, 2, width, width), F32),
            pltpu.VMEM((count, 2, width, width), F32),
            pltpu.VMEM((count, 2, width, width), F32),
            pltpu.VMEM((count, 2, width, width), F32),
            pltpu.VMEM((2 * REACH, 2, width, width), F32),
            dma((count,)), dma((count,)), dma((count,)), dma((count,)),
            dma((2 * REACH,)), dma((2 * REACH,)),
        ],
        compiler_params=pltpu.CompilerParams(
            collective_id=0, has_side_effects=True, vmem_limit_bytes=60 * 2**20
        ),
    )(energies, offsets, strength, self_in, onsite, within, between, coupling, groups)


def solution(mesh):
    placed = (
        P("energy", "section", None, None, None),
        P("section", None),
        P("section", None, None),
        P("section", None, None),
        P("section", None, None),
        P("section", None),
        P(),
        P(),
    )
    return jax.shard_map(
        per_device,
        mesh=mesh,
        in_specs=placed,
        out_specs=(
            P("energy", "section", None, None, None),
            P("energy", "section", None, None, None),
        ),
        check_vma=False,
    )
```

```python
import functools

import jax
import jax.numpy as jnp
from jax import lax
from jax.experimental import pallas as pl
from jax.experimental.pallas import tpu as pltpu
from jax.sharding import PartitionSpec as P

NEWTON = 3
ETA = 1.0
CONTACT = 0.6
REACH = 2
CHUNKS = 2

F32 = jnp.float32
BF16 = jnp.bfloat16
MESH = pl.DeviceIdType.MESH


def split(value):
    high = value.astype(BF16)
    return high, (value - high.astype(F32)).astype(BF16)


def join(pieces, axis):
    return tuple(jnp.concatenate(parts, axis=axis) for parts in zip(*pieces))


def dot(left, right):
    return jnp.dot(left, right, preferred_element_type=F32)


def matmul(left, right):
    (left_h, left_l), (right_h, right_l) = left, right
    return dot(left_h, right_h) + (dot(left_h, right_l) + dot(left_l, right_h))


def minus(pair):
    return tuple(-part for part in pair)


def complex_product(left, right):
    size = left[0][0].shape[0]
    rows = join(left, 1)
    columns = join([join([right[0], right[1]], 1), join([minus(right[1]), right[0]], 1)], 0)
    result = matmul(rows, columns)
    return result[:, :size], result[:, size:]


def complex_columns(block):
    return join([join([block[0], block[1]], 1), join([minus(block[1]), block[0]], 1)], 0)


def rows_of(pair, start, size):
    return tuple(part[start : start + size] for part in pair)


def congruence(first, field, second):
    size = first[0].shape[0]
    half = matmul(join(field, 0), second)
    half = join([split(half[:size]), split(half[size:])], 1)
    result = matmul(first, half)
    return result[:, :size], result[:, size:]


def kernel(
    energies, offsets, strength, self_in, onsite, within, between, coupling, groups,
    green, self_out,
    hamil, hops, mats, local, came_f, came_b, sent_b, halo,
    send_f, recv_f, send_b, recv_b, send_h, recv_h, token,
):
    count, width = self_in.shape[0], self_in.shape[3]
    sections, place = lax.axis_size("section"), lax.axis_index("section")
    spans, seat = lax.axis_size("energy"), lax.axis_index("energy")
    has_prev, has_next = place > 0, place < sections - 1
    has_low, has_high = seat > 0, seat < spans - 1
    last = sections - 1
    chunk = width // CHUNKS
    odd = lax.rem(seat, 2) == 1
    partner = jnp.where(odd, seat - 1, seat + 1)
    paced = (place == 0) & has_next & (odd | has_high)

    barrier = pltpu.get_barrier_semaphore()
    for present, target in (
        (has_prev, {"section": place - 1}),
        (has_next, {"section": place + 1}),
        (has_low, {"energy": seat - 1}),
        (has_high, {"energy": seat + 1}),
    ):
        @pl.when(present)
        def _():
            pl.semaphore_signal(barrier, inc=1, device_id=target, device_id_type=MESH)

    eye = (
        lax.broadcasted_iota(jnp.int32, (width, width), 0)
        == lax.broadcasted_iota(jnp.int32, (width, width), 1)
    )
    hamil[...] = jnp.where(eye, onsite[0:1, :], 0.0) + 0.5 * (within[0] + within[0].T)
    hop = between[0]
    hops[0], hops[1] = split(hop)
    hops[2], hops[3] = split(hop.T)
    row_group = jnp.broadcast_to(groups[0:1, :].astype(F32), (width, width))
    mat = jnp.where(row_group == row_group.T, coupling[0], 0.0)
    mats[0], mats[1] = split(mat)
    mats[2], mats[3] = split(mat.T)

    @pl.when(place == 0)
    def _():
        for index in range(count):
            came_f[index, 0] = jnp.zeros((width, width), F32)
            came_f[index, 1] = jnp.where(eye, -CONTACT, 0.0)

    @pl.when(seat == 0)
    def _():
        halo[0:REACH] = jnp.zeros((REACH, 2, width, width), F32)

    @pl.when(seat == spans - 1)
    def _():
        halo[REACH : 2 * REACH] = jnp.zeros((REACH, 2, width, width), F32)

    peers = sum(present.astype(jnp.int32) for present in (has_prev, has_next, has_low, has_high))
    pl.semaphore_wait(barrier, peers)

    def forward_copy(index, piece):
        rows = pl.ds(piece * chunk, chunk)
        return pltpu.make_async_remote_copy(
            src_ref=local.at[index, :, rows], dst_ref=came_f.at[index, :, rows],
            send_sem=send_f.at[index, piece], recv_sem=recv_f.at[index, piece],
            device_id={"section": place + 1}, device_id_type=MESH,
        )

    def backward_copy(index, piece):
        rows = pl.ds(piece * chunk, chunk)
        return pltpu.make_async_remote_copy(
            src_ref=sent_b.at[index, :, rows], dst_ref=came_b.at[index, :, rows],
            send_sem=send_b.at[index, piece], recv_sem=recv_b.at[index, piece],
            device_id={"section": place - 1}, device_id_type=MESH,
        )

    def halo_up(index):
        slot = index - (count - REACH)
        return pltpu.make_async_remote_copy(
            src_ref=green.at[index, 0], dst_ref=halo.at[slot],
            send_sem=send_h.at[slot], recv_sem=recv_h.at[slot],
            device_id={"energy": seat + 1}, device_id_type=MESH,
        )

    def halo_down(index):
        slot = index + REACH
        return pltpu.make_async_remote_copy(
            src_ref=green.at[index, 0], dst_ref=halo.at[slot],
            send_sem=send_h.at[slot], recv_sem=recv_h.at[slot],
            device_id={"energy": seat - 1}, device_id_type=MESH,
        )

    def forward(index):
        halves = []
        for piece in range(CHUNKS):
            @pl.when(has_prev)
            def _():
                forward_copy(index, piece).wait_recv()

            rows = slice(piece * chunk, (piece + 1) * chunk)
            field = [split(came_f[index, part, rows]) for part in range(2)]
            half = matmul(join(field, 0), (hops[0], hops[1]))
            halves.append(join([split(half[:chunk]), split(half[chunk:])], 1))
        left = matmul((hops[2], hops[3]), join(halves, 0))
        left_re, left_im = left[:, :width], left[:, width:]
        sys_re = jnp.where(eye, energies[index], 0.0) - hamil[...] - self_in[index, 0, 0] - left_re
        sys_im = jnp.where(eye, ETA, 0.0) - self_in[index, 0, 1] - left_im
        diag_re = jnp.where(eye, sys_re, 0.0)
        diag_im = jnp.where(eye, sys_im, 0.0)
        inverses = []
        for axis in (1, 0):
            real_c = jnp.sum(diag_re, axis=axis, keepdims=True)
            imag_c = jnp.sum(diag_im, axis=axis, keepdims=True)
            modulus = real_c * real_c + imag_c * imag_c
            inverses.append((real_c / modulus, -imag_c / modulus))
        (col_re, col_im), (row_re, row_im) = inverses
        half_re = col_re * sys_re - col_im * sys_im
        half_im = col_re * sys_im + col_im * sys_re
        it_re = jnp.where(eye, 2.0 * col_re, 0.0) - (half_re * row_re - half_im * row_im)
        it_im = jnp.where(eye, 2.0 * col_im, 0.0) - (half_re * row_im + half_im * row_re)
        system = (split(sys_re), split(sys_im))
        for sweep in range(NEWTON - 1):
            iterate = (split(it_re), split(it_im))
            mid_re, mid_im = complex_product(system, iterate)
            columns = complex_columns((split(mid_re), split(mid_im)))
            if sweep < NEWTON - 2:
                out = matmul(join(iterate, 1), columns)
                it_re, it_im = 2.0 * it_re - out[:, :width], 2.0 * it_im - out[:, width:]
                continue
            rows_all = join(iterate, 1)
            for piece in range(CHUNKS):
                rows = slice(piece * chunk, (piece + 1) * chunk)
                out = matmul(rows_of(rows_all, piece * chunk, chunk), columns)
                local[index, 0, rows] = 2.0 * it_re[rows] - out[:, :width]
                local[index, 1, rows] = 2.0 * it_im[rows] - out[:, width:]

                @pl.when(has_next & jnp.logical_not(paced))
                def _():
                    forward_copy(index, piece).start()

        @pl.when(paced)
        def _():
            @pl.when(odd | (index > 0))
            def _():
                pl.semaphore_wait(token, 1)

            for piece in range(CHUNKS):
                forward_copy(index, piece).start()
            for piece in range(CHUNKS - 1):
                forward_copy(index, piece).wait_send()

            @pl.when(jnp.logical_not(odd) | (index < count - 1))
            def _():
                pl.semaphore_signal(
                    token, inc=1, device_id={"energy": partner}, device_id_type=MESH
                )

    def backward(index):
        @pl.when(has_next)
        def _():
            base_re, base_im = local[index, 0], local[index, 1]
            base = (split(base_re), split(base_im))
            columns = complex_columns(base)
            mids = []
            for piece in range(CHUNKS):
                backward_copy(index, piece).wait_recv()
                rows = slice(piece * chunk, (piece + 1) * chunk)
                incoming = join([split(came_b[index, part, rows]) for part in range(2)], 1)
                mids.append(matmul(incoming, columns))
            mid = jnp.concatenate(mids, axis=0)
            out_re, out_im = complex_product(base, (split(mid[:, :width]), split(mid[:, width:])))
            green[index, 0, 0] = base_re + out_re
            green[index, 0, 1] = base_im + out_im

        @pl.when(place == last)
        def _():
            green[index, 0] = local[index]

        @pl.when(has_prev)
        def _():
            field = join([split(green[index, 0, part]) for part in range(2)], 1)
            for piece in range(CHUNKS):
                rows = slice(piece * chunk, (piece + 1) * chunk)
                half = matmul((hops[0, rows], hops[1, rows]), field)
                half = join([split(half[:, :width]), split(half[:, width:])], 0)
                out = matmul(half, (hops[2], hops[3]))
                sent_b[index, 0, rows] = out[:chunk]
                sent_b[index, 1, rows] = out[chunk:]
                backward_copy(index, piece).start()

        @pl.when(has_high & (index >= count - REACH))
        def _():
            halo_up(index).start()

        @pl.when(has_low & (index < REACH))
        def _():
            halo_down(index).start()

    def turn(step, carry):
        ahead = step - place
        back = step - 2 * last + place

        @pl.when((ahead >= 0) & (ahead < count))
        def _():
            forward(ahead)

        @pl.when((back >= 0) & (back < count))
        def _():
            backward(back)

        return carry

    lax.fori_loop(0, count + 2 * last, turn, 0)

    near = jnp.float32(0.0)
    far = jnp.float32(0.0)
    for mode in range(offsets.shape[0]):
        near = near + jnp.where(offsets[mode] == 1, strength[mode], 0.0)
        far = far + jnp.where(offsets[mode] == 2, strength[mode], 0.0)

    @pl.when(has_high)
    def _():
        for slot in range(REACH):
            halo_down(slot).wait_recv()

    def block(index, part):
        if index < 0:
            return halo[index + REACH, part]
        if index >= count:
            return halo[index - count + REACH, part]
        return green[index, 0, part]

    first, second = (mats[0], mats[1]), (mats[2], mats[3])
    waited = [False]
    for index in reversed(range(count)):
        if index < REACH and not waited[0]:
            waited[0] = True

            @pl.when(has_low)
            def _():
                for slot in range(REACH):
                    halo_up(count - REACH + slot).wait_recv()

        field = tuple(
            split(
                near * (block(index - 1, part) + block(index + 1, part))
                + far * (block(index - 2, part) + block(index + 2, part))
            )
            for part in range(2)
        )
        out_re, out_im = congruence(first, field, second)
        self_out[index, 0, 0] = out_re
        self_out[index, 0, 1] = out_im

    @pl.when(has_next)
    def _():
        for index in range(count):
            for piece in range(CHUNKS - 1):
                @pl.when(jnp.logical_not(paced))
                def _():
                    forward_copy(index, piece).wait_send()

            forward_copy(index, CHUNKS - 1).wait_send()

    @pl.when(has_prev)
    def _():
        for index in range(count):
            for piece in range(CHUNKS):
                backward_copy(index, piece).wait_send()

    @pl.when(has_high)
    def _():
        for slot in range(REACH):
            halo_up(count - REACH + slot).wait_send()

    @pl.when(has_low)
    def _():
        for slot in range(REACH):
            halo_down(slot).wait_send()


def per_device(self_in, onsite, within, between, coupling, groups, offsets, strength):
    count, width = self_in.shape[0], self_in.shape[3]
    total = count * lax.axis_size("energy")
    first_index = lax.axis_index("energy") * count
    energies = (
        -1.0
        + (2 * (first_index + jnp.arange(count, dtype=jnp.int32)) + 1).astype(jnp.float32) / total
    )
    smem = pl.BlockSpec(memory_space=pltpu.SMEM)
    vmem = pl.BlockSpec(memory_space=pltpu.VMEM)
    shape = jax.ShapeDtypeStruct(self_in.shape, F32)
    dma = pltpu.SemaphoreType.DMA
    return pl.pallas_call(
        kernel,
        out_shape=(shape, shape),
        in_specs=[smem] * 3 + [vmem] * 6,
        out_specs=(vmem, vmem),
        scratch_shapes=[
            pltpu.VMEM((width, width), F32),
            pltpu.VMEM((4, width, width), BF16),
            pltpu.VMEM((4, width, width), BF16),
            pltpu.VMEM((count, 2, width, width), F32),
            pltpu.VMEM((count, 2, width, width), F32),
            pltpu.VMEM((count, 2, width, width), F32),
            pltpu.VMEM((count, 2, width, width), F32),
            pltpu.VMEM((2 * REACH, 2, width, width), F32),
            dma((count, CHUNKS)), dma((count, CHUNKS)), dma((count, CHUNKS)), dma((count, CHUNKS)),
            dma((2 * REACH,)), dma((2 * REACH,)), pltpu.SemaphoreType.REGULAR,
        ],
        compiler_params=pltpu.CompilerParams(
            collective_id=0, has_side_effects=True, vmem_limit_bytes=60 * 2**20
        ),
    )(energies, offsets, strength, self_in, onsite, within, between, coupling, groups)


def solution(mesh):
    placed = (
        P("energy", "section", None, None, None),
        P("section", None),
        P("section", None, None),
        P("section", None, None),
        P("section", None, None),
        P("section", None),
        P(),
        P(),
    )
    return jax.shard_map(
        per_device,
        mesh=mesh,
        in_specs=placed,
        out_specs=(
            P("energy", "section", None, None, None),
            P("energy", "section", None, None, None),
        ),
        check_vma=False,
    )
```

```python
import functools

import jax
import jax.numpy as jnp
from jax import lax
from jax.experimental import pallas as pl
from jax.experimental.pallas import tpu as pltpu
from jax.sharding import PartitionSpec as P

NEWTON = 3
ETA = 1.0
CONTACT = 0.6
REACH = 2
CHUNKS = 2

F32 = jnp.float32
BF16 = jnp.bfloat16
MESH = pl.DeviceIdType.MESH


def split(value):
    high = value.astype(BF16)
    return high, (value - high.astype(F32)).astype(BF16)


def join(pieces, axis):
    return tuple(jnp.concatenate(parts, axis=axis) for parts in zip(*pieces))


def dot(left, right):
    return jnp.dot(left, right, preferred_element_type=F32)


def matmul(left, right):
    (left_h, left_l), (right_h, right_l) = left, right
    return dot(left_h, right_h) + (dot(left_h, right_l) + dot(left_l, right_h))


def minus(pair):
    return tuple(-part for part in pair)


def complex_product(left, right):
    size = left[0][0].shape[0]
    rows = join(left, 1)
    columns = join([join([right[0], right[1]], 1), join([minus(right[1]), right[0]], 1)], 0)
    result = matmul(rows, columns)
    return result[:, :size], result[:, size:]


def complex_columns(block):
    return join([join([block[0], block[1]], 1), join([minus(block[1]), block[0]], 1)], 0)


def rows_of(pair, start, size):
    return tuple(part[start : start + size] for part in pair)


def congruence(first, field, second):
    size = first[0].shape[0]
    half = matmul(join(field, 0), second)
    half = join([split(half[:size]), split(half[size:])], 1)
    result = matmul(first, half)
    return result[:, :size], result[:, size:]


def kernel(
    energies, offsets, strength, self_in, onsite, within, between, coupling, groups,
    green, self_out,
    hamil, hops, mats, local, came_f, came_b, sent_b, halo,
    send_f, recv_f, send_b, recv_b, send_h, recv_h,
):
    count, width = self_in.shape[0], self_in.shape[3]
    sections, place = lax.axis_size("section"), lax.axis_index("section")
    spans, seat = lax.axis_size("energy"), lax.axis_index("energy")
    has_prev, has_next = place > 0, place < sections - 1
    has_low, has_high = seat > 0, seat < spans - 1
    last = sections - 1
    chunk = width // CHUNKS
    odd = lax.rem(seat, 2) == 1

    barrier = pltpu.get_barrier_semaphore()
    for present, target in (
        (has_prev, {"section": place - 1}),
        (has_next, {"section": place + 1}),
        (has_low, {"energy": seat - 1}),
        (has_high, {"energy": seat + 1}),
    ):
        @pl.when(present)
        def _():
            pl.semaphore_signal(barrier, inc=1, device_id=target, device_id_type=MESH)

    eye = (
        lax.broadcasted_iota(jnp.int32, (width, width), 0)
        == lax.broadcasted_iota(jnp.int32, (width, width), 1)
    )
    hamil[...] = jnp.where(eye, onsite[0:1, :], 0.0) + 0.5 * (within[0] + within[0].T)
    hop = between[0]
    hops[0], hops[1] = split(hop)
    hops[2], hops[3] = split(hop.T)
    row_group = jnp.broadcast_to(groups[0:1, :].astype(F32), (width, width))
    mat = jnp.where(row_group == row_group.T, coupling[0], 0.0)
    mats[0], mats[1] = split(mat)
    mats[2], mats[3] = split(mat.T)

    @pl.when(place == 0)
    def _():
        for index in range(count):
            came_f[index, 0] = jnp.zeros((width, width), F32)
            came_f[index, 1] = jnp.where(eye, -CONTACT, 0.0)

    @pl.when(seat == 0)
    def _():
        halo[0:REACH] = jnp.zeros((REACH, 2, width, width), F32)

    @pl.when(seat == spans - 1)
    def _():
        halo[REACH : 2 * REACH] = jnp.zeros((REACH, 2, width, width), F32)

    peers = sum(present.astype(jnp.int32) for present in (has_prev, has_next, has_low, has_high))
    pl.semaphore_wait(barrier, peers)

    def forward_copy(index, piece):
        rows = pl.ds(piece * chunk, chunk)
        return pltpu.make_async_remote_copy(
            src_ref=local.at[index, :, rows], dst_ref=came_f.at[index, :, rows],
            send_sem=send_f.at[index, piece], recv_sem=recv_f.at[index, piece],
            device_id={"section": place + 1}, device_id_type=MESH,
        )

    def backward_copy(index, piece):
        rows = pl.ds(piece * chunk, chunk)
        return pltpu.make_async_remote_copy(
            src_ref=sent_b.at[index, :, rows], dst_ref=came_b.at[index, :, rows],
            send_sem=send_b.at[index, piece], recv_sem=recv_b.at[index, piece],
            device_id={"section": place - 1}, device_id_type=MESH,
        )

    def halo_up(index):
        slot = index - (count - REACH)
        return pltpu.make_async_remote_copy(
            src_ref=green.at[index, 0], dst_ref=halo.at[slot],
            send_sem=send_h.at[slot], recv_sem=recv_h.at[slot],
            device_id={"energy": seat + 1}, device_id_type=MESH,
        )

    def halo_down(index):
        slot = index + REACH
        return pltpu.make_async_remote_copy(
            src_ref=green.at[index, 0], dst_ref=halo.at[slot],
            send_sem=send_h.at[slot], recv_sem=recv_h.at[slot],
            device_id={"energy": seat - 1}, device_id_type=MESH,
        )

    def forward(index):
        halves = []
        for piece in range(CHUNKS):
            @pl.when(has_prev)
            def _():
                forward_copy(index, piece).wait_recv()

            rows = slice(piece * chunk, (piece + 1) * chunk)
            field = [split(came_f[index, part, rows]) for part in range(2)]
            half = matmul(join(field, 0), (hops[0], hops[1]))
            halves.append(join([split(half[:chunk]), split(half[chunk:])], 1))
        left = matmul((hops[2], hops[3]), join(halves, 0))
        left_re, left_im = left[:, :width], left[:, width:]
        sys_re = jnp.where(eye, energies[index], 0.0) - hamil[...] - self_in[index, 0, 0] - left_re
        sys_im = jnp.where(eye, ETA, 0.0) - self_in[index, 0, 1] - left_im
        diag_re = jnp.where(eye, sys_re, 0.0)
        diag_im = jnp.where(eye, sys_im, 0.0)
        inverses = []
        for axis in (1, 0):
            real_c = jnp.sum(diag_re, axis=axis, keepdims=True)
            imag_c = jnp.sum(diag_im, axis=axis, keepdims=True)
            modulus = real_c * real_c + imag_c * imag_c
            inverses.append((real_c / modulus, -imag_c / modulus))
        (col_re, col_im), (row_re, row_im) = inverses
        half_re = col_re * sys_re - col_im * sys_im
        half_im = col_re * sys_im + col_im * sys_re
        it_re = jnp.where(eye, 2.0 * col_re, 0.0) - (half_re * row_re - half_im * row_im)
        it_im = jnp.where(eye, 2.0 * col_im, 0.0) - (half_re * row_im + half_im * row_re)
        system = (split(sys_re), split(sys_im))
        for sweep in range(NEWTON - 1):
            iterate = (split(it_re), split(it_im))
            mid_re, mid_im = complex_product(system, iterate)
            columns = complex_columns((split(mid_re), split(mid_im)))
            if sweep < NEWTON - 2:
                out = matmul(join(iterate, 1), columns)
                it_re, it_im = 2.0 * it_re - out[:, :width], 2.0 * it_im - out[:, width:]
                continue
            rows_all = join(iterate, 1)
            for piece in range(CHUNKS):
                rows = slice(piece * chunk, (piece + 1) * chunk)
                out = matmul(rows_of(rows_all, piece * chunk, chunk), columns)
                local[index, 0, rows] = 2.0 * it_re[rows] - out[:, :width]
                local[index, 1, rows] = 2.0 * it_im[rows] - out[:, width:]

                @pl.when(has_next)
                def _():
                    forward_copy(index, piece).start()

    def backward(index):
        @pl.when(has_next)
        def _():
            base_re, base_im = local[index, 0], local[index, 1]
            base = (split(base_re), split(base_im))
            columns = complex_columns(base)
            mids = []
            for piece in range(CHUNKS):
                backward_copy(index, piece).wait_recv()
                rows = slice(piece * chunk, (piece + 1) * chunk)
                incoming = join([split(came_b[index, part, rows]) for part in range(2)], 1)
                mids.append(matmul(incoming, columns))
            mid = jnp.concatenate(mids, axis=0)
            out_re, out_im = complex_product(base, (split(mid[:, :width]), split(mid[:, width:])))
            green[index, 0, 0] = base_re + out_re
            green[index, 0, 1] = base_im + out_im

        @pl.when(place == last)
        def _():
            green[index, 0] = local[index]

        @pl.when(has_prev)
        def _():
            field = join([split(green[index, 0, part]) for part in range(2)], 1)
            for piece in range(CHUNKS):
                rows = slice(piece * chunk, (piece + 1) * chunk)
                half = matmul((hops[0, rows], hops[1, rows]), field)
                half = join([split(half[:, :width]), split(half[:, width:])], 0)
                out = matmul(half, (hops[2], hops[3]))
                sent_b[index, 0, rows] = out[:chunk]
                sent_b[index, 1, rows] = out[chunk:]
                backward_copy(index, piece).start()

        @pl.when(has_high & (index >= count - REACH))
        def _():
            halo_up(index).start()

        @pl.when(has_low & (index < REACH))
        def _():
            halo_down(index).start()

    def turn(step, carry):
        ahead = step - place
        back = step - 2 * last + place

        @pl.when((ahead >= 0) & (ahead < count))
        def _():
            forward(jnp.where(odd, count - 1 - ahead, ahead))

        @pl.when((back >= 0) & (back < count))
        def _():
            backward(jnp.where(odd, count - 1 - back, back))

        return carry

    lax.fori_loop(0, count + 2 * last, turn, 0)

    near = jnp.float32(0.0)
    far = jnp.float32(0.0)
    for mode in range(offsets.shape[0]):
        near = near + jnp.where(offsets[mode] == 1, strength[mode], 0.0)
        far = far + jnp.where(offsets[mode] == 2, strength[mode], 0.0)

    @pl.when(has_high)
    def _():
        for slot in range(REACH):
            halo_down(slot).wait_recv()

    def block(index, part):
        if index < 0:
            return halo[index + REACH, part]
        if index >= count:
            return halo[index - count + REACH, part]
        return green[index, 0, part]

    first, second = (mats[0], mats[1]), (mats[2], mats[3])
    waited = [False]
    for index in reversed(range(count)):
        if index < REACH and not waited[0]:
            waited[0] = True

            @pl.when(has_low)
            def _():
                for slot in range(REACH):
                    halo_up(count - REACH + slot).wait_recv()

        field = tuple(
            split(
                near * (block(index - 1, part) + block(index + 1, part))
                + far * (block(index - 2, part) + block(index + 2, part))
            )
            for part in range(2)
        )
        out_re, out_im = congruence(first, field, second)
        self_out[index, 0, 0] = out_re
        self_out[index, 0, 1] = out_im

    @pl.when(has_next)
    def _():
        for index in range(count):
            for piece in range(CHUNKS):
                forward_copy(index, piece).wait_send()

    @pl.when(has_prev)
    def _():
        for index in range(count):
            for piece in range(CHUNKS):
                backward_copy(index, piece).wait_send()

    @pl.when(has_high)
    def _():
        for slot in range(REACH):
            halo_up(count - REACH + slot).wait_send()

    @pl.when(has_low)
    def _():
        for slot in range(REACH):
            halo_down(slot).wait_send()


def per_device(self_in, onsite, within, between, coupling, groups, offsets, strength):
    count, width = self_in.shape[0], self_in.shape[3]
    total = count * lax.axis_size("energy")
    first_index = lax.axis_index("energy") * count
    energies = (
        -1.0
        + (2 * (first_index + jnp.arange(count, dtype=jnp.int32)) + 1).astype(jnp.float32) / total
    )
    smem = pl.BlockSpec(memory_space=pltpu.SMEM)
    vmem = pl.BlockSpec(memory_space=pltpu.VMEM)
    shape = jax.ShapeDtypeStruct(self_in.shape, F32)
    dma = pltpu.SemaphoreType.DMA
    return pl.pallas_call(
        kernel,
        out_shape=(shape, shape),
        in_specs=[smem] * 3 + [vmem] * 6,
        out_specs=(vmem, vmem),
        scratch_shapes=[
            pltpu.VMEM((width, width), F32),
            pltpu.VMEM((4, width, width), BF16),
            pltpu.VMEM((4, width, width), BF16),
            pltpu.VMEM((count, 2, width, width), F32),
            pltpu.VMEM((count, 2, width, width), F32),
            pltpu.VMEM((count, 2, width, width), F32),
            pltpu.VMEM((count, 2, width, width), F32),
            pltpu.VMEM((2 * REACH, 2, width, width), F32),
            dma((count, CHUNKS)), dma((count, CHUNKS)), dma((count, CHUNKS)), dma((count, CHUNKS)),
            dma((2 * REACH,)), dma((2 * REACH,)),
        ],
        compiler_params=pltpu.CompilerParams(
            collective_id=0, has_side_effects=True, vmem_limit_bytes=60 * 2**20
        ),
    )(energies, offsets, strength, self_in, onsite, within, between, coupling, groups)


def solution(mesh):
    placed = (
        P("energy", "section", None, None, None),
        P("section", None),
        P("section", None, None),
        P("section", None, None),
        P("section", None, None),
        P("section", None),
        P(),
        P(),
    )
    return jax.shard_map(
        per_device,
        mesh=mesh,
        in_specs=placed,
        out_specs=(
            P("energy", "section", None, None, None),
            P("energy", "section", None, None, None),
        ),
        check_vma=False,
    )
```

```python
import functools

import jax
import jax.numpy as jnp
from jax import lax
from jax.experimental import pallas as pl
from jax.experimental.pallas import tpu as pltpu
from jax.sharding import PartitionSpec as P

NEWTON = 3
ETA = 1.0
CONTACT = 0.6
REACH = 2
CHUNKS = 2

F32 = jnp.float32
BF16 = jnp.bfloat16
MESH = pl.DeviceIdType.MESH


def split(value):
    high = value.astype(BF16)
    return high, (value - high.astype(F32)).astype(BF16)


def join(pieces, axis):
    return tuple(jnp.concatenate(parts, axis=axis) for parts in zip(*pieces))


def dot(left, right):
    return jnp.dot(left, right, preferred_element_type=F32)


def matmul(left, right):
    (left_h, left_l), (right_h, right_l) = left, right
    return dot(left_h, right_h) + (dot(left_h, right_l) + dot(left_l, right_h))


def minus(pair):
    return tuple(-part for part in pair)


def complex_product(left, right):
    size = left[0][0].shape[0]
    rows = join(left, 1)
    columns = join([join([right[0], right[1]], 1), join([minus(right[1]), right[0]], 1)], 0)
    result = matmul(rows, columns)
    return result[:, :size], result[:, size:]


def complex_columns(block):
    return join([join([block[0], block[1]], 1), join([minus(block[1]), block[0]], 1)], 0)


def rows_of(pair, start, size):
    return tuple(part[start : start + size] for part in pair)


def congruence(first, field, second):
    size = first[0].shape[0]
    half = matmul(join(field, 0), second)
    half = join([split(half[:size]), split(half[size:])], 1)
    result = matmul(first, half)
    return result[:, :size], result[:, size:]


def kernel(
    offsets, strength, self_in, onsite, within, between, coupling, groups,
    green, self_out,
    hamil, hops, mats, local, came_f, came_b, sent_b, halo,
    send_f, recv_f, send_b, recv_b, send_h, recv_h,
):
    count, width = self_in.shape[0], self_in.shape[3]
    sections, place = lax.axis_size("section"), lax.axis_index("section")
    spans, seat = lax.axis_size("energy"), lax.axis_index("energy")
    has_prev, has_next = place > 0, place < sections - 1
    has_low, has_high = seat > 0, seat < spans - 1
    last = sections - 1
    chunk = width // CHUNKS
    odd = lax.rem(seat, 2) == 1

    barrier = pltpu.get_barrier_semaphore()
    for present, target in (
        (has_prev, {"section": place - 1}),
        (has_next, {"section": place + 1}),
        (has_low, {"energy": seat - 1}),
        (has_high, {"energy": seat + 1}),
    ):
        @pl.when(present)
        def _():
            pl.semaphore_signal(barrier, inc=1, device_id=target, device_id_type=MESH)

    eye = (
        lax.broadcasted_iota(jnp.int32, (width, width), 0)
        == lax.broadcasted_iota(jnp.int32, (width, width), 1)
    )
    hamil[...] = jnp.where(eye, onsite[0:1, :], 0.0) + 0.5 * (within[0] + within[0].T)
    hop = between[0]
    hops[0], hops[1] = split(hop)
    hops[2], hops[3] = split(hop.T)
    row_group = jnp.broadcast_to(groups[0:1, :].astype(F32), (width, width))
    mat = jnp.where(row_group == row_group.T, coupling[0], 0.0)
    mats[0], mats[1] = split(mat)
    mats[2], mats[3] = split(mat.T)

    @pl.when(place == 0)
    def _():
        for index in range(count):
            came_f[index, 0] = jnp.zeros((width, width), F32)
            came_f[index, 1] = jnp.where(eye, -CONTACT, 0.0)

    @pl.when(seat == 0)
    def _():
        halo[0:REACH] = jnp.zeros((REACH, 2, width, width), F32)

    @pl.when(seat == spans - 1)
    def _():
        halo[REACH : 2 * REACH] = jnp.zeros((REACH, 2, width, width), F32)

    peers = sum(present.astype(jnp.int32) for present in (has_prev, has_next, has_low, has_high))
    pl.semaphore_wait(barrier, peers)

    def forward_copy(index, piece):
        rows = pl.ds(piece * chunk, chunk)
        return pltpu.make_async_remote_copy(
            src_ref=local.at[index, :, rows], dst_ref=came_f.at[index, :, rows],
            send_sem=send_f.at[index, piece], recv_sem=recv_f.at[index, piece],
            device_id={"section": place + 1}, device_id_type=MESH,
        )

    def backward_copy(index, piece):
        rows = pl.ds(piece * chunk, chunk)
        return pltpu.make_async_remote_copy(
            src_ref=sent_b.at[index, :, rows], dst_ref=came_b.at[index, :, rows],
            send_sem=send_b.at[index, piece], recv_sem=recv_b.at[index, piece],
            device_id={"section": place - 1}, device_id_type=MESH,
        )

    def halo_up(index):
        slot = index - (count - REACH)
        return pltpu.make_async_remote_copy(
            src_ref=green.at[index, 0], dst_ref=halo.at[slot],
            send_sem=send_h.at[slot], recv_sem=recv_h.at[slot],
            device_id={"energy": seat + 1}, device_id_type=MESH,
        )

    def halo_down(index):
        slot = index + REACH
        return pltpu.make_async_remote_copy(
            src_ref=green.at[index, 0], dst_ref=halo.at[slot],
            send_sem=send_h.at[slot], recv_sem=recv_h.at[slot],
            device_id={"energy": seat - 1}, device_id_type=MESH,
        )

    def forward(index):
        halves = []
        for piece in range(CHUNKS):
            @pl.when(has_prev)
            def _():
                forward_copy(index, piece).wait_recv()

            rows = slice(piece * chunk, (piece + 1) * chunk)
            field = [split(came_f[index, part, rows]) for part in range(2)]
            half = matmul(join(field, 0), (hops[0], hops[1]))
            halves.append(join([split(half[:chunk]), split(half[chunk:])], 1))
        left = matmul((hops[2], hops[3]), join(halves, 0))
        left_re, left_im = left[:, :width], left[:, width:]
        number = jnp.full((1, width), 2 * (seat * count + index) + 1, jnp.int32)
        energy = -1.0 + number.astype(F32) / (count * spans)
        sys_re = jnp.where(eye, energy, 0.0) - hamil[...] - self_in[index, 0, 0] - left_re
        sys_im = jnp.where(eye, ETA, 0.0) - self_in[index, 0, 1] - left_im
        diag_re = jnp.where(eye, sys_re, 0.0)
        diag_im = jnp.where(eye, sys_im, 0.0)
        inverses = []
        for axis in (1, 0):
            real_c = jnp.sum(diag_re, axis=axis, keepdims=True)
            imag_c = jnp.sum(diag_im, axis=axis, keepdims=True)
            modulus = real_c * real_c + imag_c * imag_c
            inverses.append((real_c / modulus, -imag_c / modulus))
        (col_re, col_im), (row_re, row_im) = inverses
        half_re = col_re * sys_re - col_im * sys_im
        half_im = col_re * sys_im + col_im * sys_re
        it_re = jnp.where(eye, 2.0 * col_re, 0.0) - (half_re * row_re - half_im * row_im)
        it_im = jnp.where(eye, 2.0 * col_im, 0.0) - (half_re * row_im + half_im * row_re)
        system = (split(sys_re), split(sys_im))
        for sweep in range(NEWTON - 1):
            iterate = (split(it_re), split(it_im))
            mid_re, mid_im = complex_product(system, iterate)
            columns = complex_columns((split(mid_re), split(mid_im)))
            if sweep < NEWTON - 2:
                out = matmul(join(iterate, 1), columns)
                it_re, it_im = 2.0 * it_re - out[:, :width], 2.0 * it_im - out[:, width:]
                continue
            rows_all = join(iterate, 1)
            for piece in range(CHUNKS):
                rows = slice(piece * chunk, (piece + 1) * chunk)
                out = matmul(rows_of(rows_all, piece * chunk, chunk), columns)
                local[index, 0, rows] = 2.0 * it_re[rows] - out[:, :width]
                local[index, 1, rows] = 2.0 * it_im[rows] - out[:, width:]

                @pl.when(has_next)
                def _():
                    forward_copy(index, piece).start()

    def backward(index):
        @pl.when(has_next)
        def _():
            base_re, base_im = local[index, 0], local[index, 1]
            base = (split(base_re), split(base_im))
            columns = complex_columns(base)
            mids = []
            for piece in range(CHUNKS):
                backward_copy(index, piece).wait_recv()
                rows = slice(piece * chunk, (piece + 1) * chunk)
                incoming = join([split(came_b[index, part, rows]) for part in range(2)], 1)
                mids.append(matmul(incoming, columns))
            mid = jnp.concatenate(mids, axis=0)
            out_re, out_im = complex_product(base, (split(mid[:, :width]), split(mid[:, width:])))
            green[index, 0, 0] = base_re + out_re
            green[index, 0, 1] = base_im + out_im

        @pl.when(place == last)
        def _():
            green[index, 0] = local[index]

        @pl.when(has_prev)
        def _():
            field = join([split(green[index, 0, part]) for part in range(2)], 1)
            for piece in range(CHUNKS):
                rows = slice(piece * chunk, (piece + 1) * chunk)
                half = matmul((hops[0, rows], hops[1, rows]), field)
                half = join([split(half[:, :width]), split(half[:, width:])], 0)
                out = matmul(half, (hops[2], hops[3]))
                sent_b[index, 0, rows] = out[:chunk]
                sent_b[index, 1, rows] = out[chunk:]
                backward_copy(index, piece).start()

        @pl.when(has_high & (index >= count - REACH))
        def _():
            halo_up(index).start()

        @pl.when(has_low & (index < REACH))
        def _():
            halo_down(index).start()

    def turn(step, carry):
        ahead = step - place
        back = step - 2 * last + place

        @pl.when((ahead >= 0) & (ahead < count))
        def _():
            forward(jnp.where(odd, count - 1 - ahead, ahead))

        @pl.when((back >= 0) & (back < count))
        def _():
            backward(jnp.where(odd, count - 1 - back, back))

        return carry

    lax.fori_loop(0, count + 2 * last, turn, 0)

    near = jnp.float32(0.0)
    far = jnp.float32(0.0)
    for mode in range(offsets.shape[0]):
        near = near + jnp.where(offsets[mode] == 1, strength[mode], 0.0)
        far = far + jnp.where(offsets[mode] == 2, strength[mode], 0.0)

    @pl.when(has_high)
    def _():
        for slot in range(REACH):
            halo_down(slot).wait_recv()

    def block(index, part):
        if index < 0:
            return halo[index + REACH, part]
        if index >= count:
            return halo[index - count + REACH, part]
        return green[index, 0, part]

    first, second = (mats[0], mats[1]), (mats[2], mats[3])
    waited = [False]
    for index in reversed(range(count)):
        if index < REACH and not waited[0]:
            waited[0] = True

            @pl.when(has_low)
            def _():
                for slot in range(REACH):
                    halo_up(count - REACH + slot).wait_recv()

        field = tuple(
            split(
                near * (block(index - 1, part) + block(index + 1, part))
                + far * (block(index - 2, part) + block(index + 2, part))
            )
            for part in range(2)
        )
        out_re, out_im = congruence(first, field, second)
        self_out[index, 0, 0] = out_re
        self_out[index, 0, 1] = out_im

    @pl.when(has_next)
    def _():
        for index in range(count):
            for piece in range(CHUNKS):
                forward_copy(index, piece).wait_send()

    @pl.when(has_prev)
    def _():
        for index in range(count):
            for piece in range(CHUNKS):
                backward_copy(index, piece).wait_send()

    @pl.when(has_high)
    def _():
        for slot in range(REACH):
            halo_up(count - REACH + slot).wait_send()

    @pl.when(has_low)
    def _():
        for slot in range(REACH):
            halo_down(slot).wait_send()


def per_device(self_in, onsite, within, between, coupling, groups, offsets, strength):
    count, width = self_in.shape[0], self_in.shape[3]
    smem = pl.BlockSpec(memory_space=pltpu.SMEM)
    vmem = pl.BlockSpec(memory_space=pltpu.VMEM)
    shape = jax.ShapeDtypeStruct(self_in.shape, F32)
    dma = pltpu.SemaphoreType.DMA
    return pl.pallas_call(
        kernel,
        out_shape=(shape, shape),
        in_specs=[smem] * 2 + [vmem] * 6,
        out_specs=(vmem, vmem),
        scratch_shapes=[
            pltpu.VMEM((width, width), F32),
            pltpu.VMEM((4, width, width), BF16),
            pltpu.VMEM((4, width, width), BF16),
            pltpu.VMEM((count, 2, width, width), F32),
            pltpu.VMEM((count, 2, width, width), F32),
            pltpu.VMEM((count, 2, width, width), F32),
            pltpu.VMEM((count, 2, width, width), F32),
            pltpu.VMEM((2 * REACH, 2, width, width), F32),
            dma((count, CHUNKS)), dma((count, CHUNKS)), dma((count, CHUNKS)), dma((count, CHUNKS)),
            dma((2 * REACH,)), dma((2 * REACH,)),
        ],
        compiler_params=pltpu.CompilerParams(
            collective_id=0, has_side_effects=True, vmem_limit_bytes=60 * 2**20
        ),
    )(offsets, strength, self_in, onsite, within, between, coupling, groups)


def solution(mesh):
    placed = (
        P("energy", "section", None, None, None),
        P("section", None),
        P("section", None, None),
        P("section", None, None),
        P("section", None, None),
        P("section", None),
        P(),
        P(),
    )
    return jax.shard_map(
        per_device,
        mesh=mesh,
        in_specs=placed,
        out_specs=(
            P("energy", "section", None, None, None),
            P("energy", "section", None, None, None),
        ),
        check_vma=False,
    )
```
